512 devices in a mesh: box: 64 (over y, z), tile: 4 (over x_lo, core), col: 2 (over x_hi).
Axes of the slice: x: 4 (x_hi: 2, x_lo: 2; x = x_hi * 2 + x_lo), y: 8, z: 8, core: 2. Of those that a mesh axis runs over, the one named last changes fastest.
Arguments:
- box_operators: float32 [4, 64, 2, 256, 512], P(None, 'box', None, 'tile', 'col'), as said below
Outputs:
- merged: float32 [4, 64, 128, 512], P(None, 'box', 'tile', 'col')
Inputs may be any that keep to these rules, and one draw needn't show every extreme that they name: `box_operators`: every box's operator is symmetric and positive definite.
All inputs are finite; a program needn't handle non-finite values.
Results may differ from the reference program's by a relative error of at most 0.0001.
Values sent between devices are 32-bit elements; how exact they have to be, the bound alone decides.
A program may use at most 64 MiB of HBM per device.

```python
import math
import jax
import jax.numpy as jnp
from jax import lax

F = 256
ROWS = 4
BOXES = 64
N_TILE = 4


def draw_box_operators(key, part):
    keys = jax.random.split(key, ROWS * BOXES)
    size_two = 2 * F
    index = jnp.arange(size_two, dtype=jnp.int32)
    face = (index // F).astype(jnp.float32)
    local = index % F
    first_coord = (local // 16).astype(jnp.float32)
    second_coord = (local % 16).astype(jnp.float32)
    depth = face * 3.0
    distance = jnp.sqrt(jnp.square(depth[:, None] - depth[None, :]) + jnp.square(first_coord[:, None] - first_coord[None, :]) + jnp.square(second_coord[:, None] - second_coord[None, :]))
    kernel = jnp.exp(-distance / 3.0)

    def single(subkey):
        key_one, key_two, key_three = jax.random.split(subkey, 3)
        noise = jax.random.uniform(key_one, (size_two, size_two), jnp.float32, -1.0, 1.0)
        noise = noise * (0.5 / math.sqrt(size_two))
        symmetric = 0.5 * (noise + noise.T)
        diagonal = jax.random.uniform(key_two, (size_two,), jnp.float32, 1.0, 4.0)
        scales = jnp.exp(jax.random.uniform(key_three, (size_two,), jnp.float32, math.log(0.5), math.log(8.0)))
        identity = jnp.eye(size_two, dtype=jnp.float32)
        matrix = kernel * scales[:, None] * scales[None, :] + symmetric + identity * diagonal[None, :]
        matrix = matrix * 0.125
        return matrix.reshape(2, F, size_two)
    result = jax.vmap(single)(keys)
    return result.reshape(ROWS, BOXES, 2, F, size_two)


def setup_inputs(seed: int = 0) -> dict:
    seeds = jax.random.split(jax.random.key(seed), 2)
    return {
        "box_operators": draw_box_operators(jax.random.fold_in(seeds[1], 71), 0),
    }


def merge_pair(left, right):
    system = left[F:, F:] + right[:F, :F]
    target = jnp.concatenate([left[F:, :F], right[:F, F:]], axis=1)
    factor = jnp.linalg.cholesky(system)
    solved = jax.scipy.linalg.cho_solve((factor, True), target)
    upper = jnp.concatenate([left[:F, :F], jnp.zeros_like(left[:F, :F])], axis=1)
    upper = upper - jnp.dot(left[:F, F:], solved, precision=lax.Precision.HIGHEST)
    lower = jnp.concatenate([jnp.zeros_like(right[F:, F:]), right[F:, F:]], axis=1)
    lower = lower - jnp.dot(right[F:, :F], solved, precision=lax.Precision.HIGHEST)
    return jnp.concatenate([upper, lower], axis=0)

def reference(box_operators):
    results = []
    half_block = F // (2 * N_TILE)
    for index in range(ROWS):
        operators = box_operators[index].reshape(BOXES // 2, 2, 2 * F, 2 * F)
        parents = lax.map(lambda pair: merge_pair(pair[0], pair[1]), operators)
        quads = parents.reshape(BOXES // 4, 2, 2 * F, 2 * F)
        grand = lax.map(lambda pair: merge_pair(pair[0], pair[1]), quads)
        shaped = grand.reshape(BOXES // 4, 2, N_TILE, 2, half_block, 2 * F)
        shaped = shaped.transpose(0, 1, 3, 2, 4, 5).reshape(BOXES, F // 2, 2 * F)
        results.append(shaped)
    return jnp.stack(results)
```

```python
import jax
import jax.numpy as jnp
from jax import lax
from jax.experimental import pallas as pl
from jax.experimental.pallas import tpu as pltpu
from jax.sharding import PartitionSpec as P

HI = lax.Precision.HIGHEST

def dot(a, b, ca=1, cb=0):
    return lax.dot_general(a, b, (((ca,), (cb,)), ((), ())), precision=HI, preferred_element_type=jnp.float32)

def leaf(cols, sub):
    cols = list(cols)
    for k in range(8):
        piv = 1.0 / jnp.broadcast_to(cols[k][k:k+1, :], (8, 128))
        here = sub == k
        ck = cols[k]
        for c in range(8):
            if c == k:
                continue
            row = jnp.broadcast_to(cols[c][k:k+1, :], (8, 128)) * piv
            cols[c] = jnp.where(here, row, cols[c] - ck * row)
        cols[k] = jnp.where(here, piv, -ck * piv)
    return cols

def treesum(xs):
    while len(xs) > 1:
        xs = [xs[i] + xs[i+1] if i + 1 < len(xs) else xs[i] for i in range(0, len(xs), 2)]
    return xs[0]

def apply8(cols, y):
    return treesum([cols[j] * jnp.broadcast_to(y[j:j+1, :], (8, 128)) for j in range(8)])

def eliminate(mats):
    sub = lax.broadcasted_iota(jnp.int32, (8, 128), 0)
    lane = lax.broadcasted_iota(jnp.int32, (8, 128), 1)
    mats = [list(m) for m in mats]
    es = [[] for _ in mats]
    des = [[] for _ in mats]
    for k in range(16):
        lo = 8 * k
        inblk = (lane >= lo) & (lane < lo + 8)
        eye = jnp.where(lane == sub + lo, 1.0, 0.0).astype(jnp.float32)
        for n, m in enumerate(mats):
            r = m[k]
            cols = leaf([jnp.broadcast_to(r[:, lo+c:lo+c+1], (8, 128)) for c in range(8)], sub)
            rm = jnp.where(inblk, eye, r)
            y = apply8(cols, rm)
            es[n].append(jnp.where(lane < lo + 8, rm, 0.0))
            des[n].append(jnp.where(lane < lo + 8, y, 0.0))
            ys = [jnp.broadcast_to(y[j:j+1, :], (8, 128)) for j in range(8)]
            for i in range(k + 1, 16):
                a = m[i]
                upd = treesum([jnp.broadcast_to(a[:, lo+j:lo+j+1], (8, 128)) * ys[j] for j in range(8)])
                m[i] = jnp.where(inblk, 0.0, a) - upd
    return es, des

def factor(mat_refs, fac_refs):
    es, des = eliminate([[m[8*i:8*i+8, :] for i in range(16)] for m in mat_refs])
    for f, e, d in zip(fac_refs, es, des):
        for i in range(16):
            f[8*i:8*i+8, :] = e[i]
            f[128+8*i:128+8*i+8, :] = d[i]

def solve(aug, fac, vs, ys, width):
    factor([a.at[0:128, 0:128] for a in aug], fac)
    for a, f, v, y in zip(aug, fac, vs, ys):
        vy = dot(f[...], a[0:128, 128:])
        v[0:128, :] = vy[0:128, 128:]
        y[0:128, :] = vy[128:, 128:]
        a[128:256, 128:] = a[128:256, 128:] - dot(vy[0:128, 0:128], vy[128:, :], 0, 0)
    factor([a.at[128:256, 128:256] for a in aug], fac)
    for a, f, v, y in zip(aug, fac, vs, ys):
        vy = dot(f[...], a[128:256, 256:])
        v[128:256, :] = vy[0:128, :]
        y[128:256, :] = vy[128:, :]

def kernel(g_ref, d_ref, o_ref, a0, a1, a2, v0, v1, v2, y0, y1, y2, f0, f1):
    tile = lax.axis_index("tile")
    col = lax.axis_index("col")
    for p, a in enumerate((a0, a1)):
        a[:, 0:256] = g_ref[0, p] + g_ref[1, p]
        a[:, 256:512] = g_ref[0, 2 + p]
        a[:, 512:768] = g_ref[1, 2 + p]
    solve((a0, a1), (f0, f1), (v0, v1), (y0, y1), 512)
    p0 = dot(v0[:, 256:512], y0[...], 0, 0)
    p1 = dot(v1[:, 0:256], y1[...], 0, 0)
    a2[:, 0:256] = g_ref[0, 4] + g_ref[1, 4] - p0[:, 256:512] - p1[:, 0:256]
    a2[:, 256:512] = -p0[:, 0:256]
    a2[:, 512:768] = -p1[:, 256:512]
    solve((a2,), (f0,), (v2,), (y2,), 512)
    start = pl.multiple_of(tile // 2 * 128, 128)
    half = tile % 2
    cols = pl.multiple_of(col * 256, 256)
    a0[:, 0:128] = v2[:, pl.ds(start, 128)]
    a0[:, 128:256] = v2[:, pl.ds(start + 256, 128)]
    a0[:, 256:512] = y2[:, pl.ds(cols, 256)]
    a1[:, 0:128] = jnp.where(col == 0, v0[:, pl.ds(start, 128)], v1[:, pl.ds(start + 256, 128)])
    a1[:, 256:512] = jnp.where(col == 0, y0[:, 0:256], y1[:, 256:512])
    a2[:, 0:256] = dot(a0[:, 0:256], a0[:, 256:512], 0, 0)
    a2[0:128, 256:512] = dot(a1[:, 0:128], a1[:, 256:512], 0, 0)
    row = pl.multiple_of(half * 64, 64)
    own = d_ref[...] - a2[pl.ds(row, 64), 256:512]
    o_ref[0:64, :] = jnp.where(col == 0, own, 0.0) - a2[pl.ds(row, 64), 0:256]
    o_ref[64:128, :] = jnp.where(col == 1, own, 0.0) - a2[pl.ds(128 + row, 64), 0:256]


def call(g, d):
    V = pltpu.VMEM
    f = jnp.float32
    return pl.pallas_call(
        kernel,
        out_shape=jax.ShapeDtypeStruct((128, 256), f),
        scratch_shapes=[V((256, 768), f)] * 3 + [V((256, 512), f)] * 6 + [V((256, 128), f)] * 2,
        compiler_params=pltpu.CompilerParams(vmem_limit_bytes=40 << 20),
    )(g, d)


def per_device(box_operators):
    x = box_operators[:, 0]
    boxes = lax.axis_size("box")
    groups = [[4 * q + b for b in range(4)] for q in range(boxes // 4)]
    parts = lax.all_to_all(x, "box", 0, 0, axis_index_groups=groups, tiled=True)
    c0 = jnp.stack([parts[1, 0], parts[3, 0], parts[0, 1], parts[2, 1], parts[2, 0]])
    c1 = jnp.stack([parts[0, 1], parts[2, 1], parts[1, 0], parts[3, 0], parts[1, 1]])
    col = lax.axis_index("col")
    mine = jnp.where(col == 0, c0, c1)
    own = jnp.where(col == 0, parts[0, 0], parts[3, 1])
    g = lax.all_gather(mine, "tile", axis=1, tiled=True)
    g = lax.all_gather(g, "col", axis=0)
    out = call(g, own)
    out = out.reshape(4, 32, 256)
    out = lax.all_to_all(out, "box", 0, 0, axis_index_groups=groups, tiled=True)
    return out[:, None]


def solution(mesh):
    return jax.shard_map(
        per_device,
        mesh=mesh,
        in_specs=(P(None, "box", None, "tile", "col"),),
        out_specs=P(None, "box", "tile", "col"),
        check_vma=False,
    )
```

```python
import jax
import jax.numpy as jnp
from jax import lax
from jax.experimental import pallas as pl
from jax.experimental.pallas import tpu as pltpu
from jax.sharding import PartitionSpec as P

HI = lax.Precision.HIGHEST

def dot(a, b, ca=1, cb=0):
    return lax.dot_general(a, b, (((ca,), (cb,)), ((), ())), precision=HI, preferred_element_type=jnp.float32)

def leaf(cols, sub):
    cols = list(cols)
    for k in range(8):
        piv = 1.0 / jnp.broadcast_to(cols[k][k:k+1, :], (8, 128))
        here = sub == k
        ck = cols[k]
        for c in range(8):
            if c == k:
                continue
            row = jnp.broadcast_to(cols[c][k:k+1, :], (8, 128)) * piv
            cols[c] = jnp.where(here, row, cols[c] - ck * row)
        cols[k] = jnp.where(here, piv, -ck * piv)
    return cols

def treesum(xs):
    while len(xs) > 1:
        xs = [xs[i] + xs[i+1] if i + 1 < len(xs) else xs[i] for i in range(0, len(xs), 2)]
    return xs[0]

def apply8(cols, y):
    return treesum([cols[j] * jnp.broadcast_to(y[j:j+1, :], (8, 128)) for j in range(8)])

def eliminate(mats):
    sub = lax.broadcasted_iota(jnp.int32, (8, 128), 0)
    lane = lax.broadcasted_iota(jnp.int32, (8, 128), 1)
    mats = [list(m) for m in mats]
    es = [[] for _ in mats]
    des = [[] for _ in mats]
    for k in range(16):
        lo = 8 * k
        inblk = (lane >= lo) & (lane < lo + 8)
        eye = jnp.where(lane == sub + lo, 1.0, 0.0).astype(jnp.float32)
        for n, m in enumerate(mats):
            r = m[k]
            cols = leaf([jnp.broadcast_to(r[:, lo+c:lo+c+1], (8, 128)) for c in range(8)], sub)
            rm = jnp.where(inblk, eye, r)
            y = apply8(cols, rm)
            es[n].append(jnp.where(lane < lo + 8, rm, 0.0))
            des[n].append(jnp.where(lane < lo + 8, y, 0.0))
            ys = [jnp.broadcast_to(y[j:j+1, :], (8, 128)) for j in range(8)]
            for i in range(k + 1, 16):
                a = m[i]
                upd = treesum([jnp.broadcast_to(a[:, lo+j:lo+j+1], (8, 128)) * ys[j] for j in range(8)])
                m[i] = jnp.where(inblk, 0.0, a) - upd
    return es, des

def factor(mat_refs, fac_refs):
    es, des = eliminate([[m[8*i:8*i+8, :] for i in range(16)] for m in mat_refs])
    for f, e, d in zip(fac_refs, es, des):
        for i in range(16):
            f[8*i:8*i+8, :] = e[i]
            f[128+8*i:128+8*i+8, :] = d[i]

def solve(a, fac, v, y):
    factor([a.at[0:128, 0:128]], [fac])
    vy = dot(fac[...], a[0:128, 128:])
    v[0:128, :] = vy[0:128, 128:]
    y[0:128, :] = vy[128:, 128:]
    a[128:256, 128:] = a[128:256, 128:] - dot(vy[0:128, 0:128], vy[128:, :], 0, 0)
    factor([a.at[128:256, 128:256]], [fac])
    vy = dot(fac[...], a[128:256, 256:])
    v[128:256, :] = vy[0:128, :]
    y[128:256, :] = vy[128:, :]


MESH = pl.DeviceIdType.MESH
SLOTS = 5


def kernel(x_ref, out_ref, g, ob, a0, a1, a2, v0, v1, v2, y0, y1, y2, f0, f1, f2, f3,
           send1, recv1, send2, recv2, sendo, recvo):
    box = lax.axis_index("box")
    tile = lax.axis_index("tile")
    col = lax.axis_index("col")
    b = box % 4
    quad = box - b
    core = tile % 2
    x = 2 * col + tile // 2
    ring = [((x + d) % 4 // 2, (x + d) % 4 % 2 * 2 + core) for d in range(4)]
    right = {"col": ring[1][0], "tile": ring[1][1]}
    left = {"col": ring[3][0], "tile": ring[3][1]}
    across = {"col": ring[2][0], "tile": ring[2][1]}
    sib = {"tile": tile + 1 - 2 * core}
    line = [{"box": quad + (b + d) % 4} for d in range(4)]

    barrier = pltpu.get_barrier_semaphore()
    for dev in (right, left, sib, line[1], line[2], line[3]):
        pl.semaphore_signal(barrier, inc=1, device_id=dev, device_id_type=MESH)
    pl.semaphore_wait(barrier, 6)

    def piece(slot, d, lo=0, n=64):
        c, t = ring[d]
        return g.at[c, slot, pl.ds(pl.multiple_of(t * 64 + lo, 32), n), :]

    def remote(src, dst, s, r, dev):
        return pltpu.make_async_remote_copy(src_ref=src, dst_ref=dst, send_sem=s, recv_sem=r,
                                            device_id=dev, device_id_type=MESH)

    def first(kind, face, slot):
        away = [remote(x_ref.at[(b + d) % 4, face], piece(slot, 0), send1.at[kind, d - 1], recv1.at[slot], line[d])
                for d in (1, 2, 3)]
        home = pltpu.make_async_copy(x_ref.at[b, face], piece(slot, 0), recv1.at[slot])
        return away, home

    is_s = col != b % 2
    own_slot = jnp.where((b == 1) | (b == 2), 4, 5)

    @pl.when(is_s)
    def _():
        away, home = first(0, col, b // 2)
        home.start()
        for c in away:
            c.start()

    @pl.when(jnp.logical_not(is_s))
    def _():
        for kind, face, slot in ((0, 1 - col, 2 + b // 2), (1, col, own_slot)):
            away, home = first(kind, face, slot)
            home.start()
            for c in away:
                c.start()

    def wait1(slot):
        pltpu.make_async_copy(piece(slot, 0), piece(slot, 0), recv1.at[slot]).wait()

    TO_R, TO_L, TO_S, FW_R, FW_L, SIB_L, SIB_R, SIB_A, SIB_B = range(9)
    via = {0: ((0, 64), None), 1: (None, (0, 64)), 2: ((0, 64), None), 3: (None, (0, 64)), 4: ((0, 32), (32, 32))}
    started = []

    def go(kind, slot, src_d, lo, n, row, dev):
        p = piece(slot, src_d, lo, n)
        c = remote(p, p, send2.at[kind, slot], recv2.at[row, slot], dev)
        c.start()
        started.append(c)

    def arrived(slot, d, lo, n, row):
        p = piece(slot, d, lo, n)
        pltpu.make_async_copy(p, p, recv2.at[row, slot]).wait()

    def s2_start(slot):
        wait1(slot)
        go(TO_R, slot, 0, 0, 64, 0, right)
        go(TO_L, slot, 0, 0, 64, 1, left)
        go(TO_S, slot, 0, 0, 64, 4, sib)

    def s2_fwd(slot):
        by_r, by_l = via[slot]
        arrived(slot, 3, 0, 64, 0)
        if by_r:
            go(FW_R, slot, 3, by_r[0], by_r[1], 2, right)
        go(SIB_L, slot, 3, 0, 64, 5, sib)
        arrived(slot, 1, 0, 64, 1)
        if by_l:
            go(FW_L, slot, 1, by_l[0], by_l[1], 3, left)
        go(SIB_R, slot, 1, 0, 64, 6, sib)

    def s2_last(slot):
        for part, row, kind, to in zip(via[slot], (2, 3), (SIB_A, SIB_B), (7, 8)):
            if part:
                arrived(slot, 2, part[0], part[1], row)
                go(kind, slot, 2, part[0], part[1], to, sib)

    def s2_done(slot):
        def other(d, lo, n, row):
            c, t = ring[d]
            p = g.at[c, slot, pl.ds(pl.multiple_of((t + 1 - 2 * core) * 64 + lo, 32), n), :]
            pltpu.make_async_copy(p, p, recv2.at[row, slot]).wait()
        other(0, 0, 64, 4)
        other(3, 0, 64, 5)
        other(1, 0, 64, 6)
        for part, row in zip(via[slot], (7, 8)):
            if part:
                other(2, part[0], part[1], row)

    for s in (0, 1):
        s2_start(s)
    for s in (0, 1):
        s2_fwd(s)
    for s in (2, 3, 4):
        s2_start(s)
    for s in (0, 1):
        s2_last(s)
    for s in (0, 1):
        s2_done(s)

    for p, a in enumerate((a0, a1)):
        a[:, 0:256] = g[0, p] + g[1, p]
    factor([a.at[0:128, 0:128] for a in (a0, a1)], [f0, f1])
    for s in (2, 3, 4):
        s2_fwd(s)
    for a, f in ((a0, f0), (a1, f1)):
        vy = dot(f[...], a[0:128, 128:256])
        a[0:128, 0:128] = vy[0:128]
        a[128:256, 128:256] = a[128:256, 128:256] - dot(vy[0:128], vy[128:], 0, 0)
    factor([a.at[128:256, 128:256] for a in (a0, a1)], [f2, f3])
    for s in (2, 3, 4):
        s2_last(s)
    for s in (2, 3, 4):
        s2_done(s)
    for p, a in enumerate((a0, a1)):
        a[:, 256:512] = g[0, 2 + p]
        a[:, 512:768] = g[1, 2 + p]
    for a, f, h, v, y in ((a0, f0, f2, v0, y0), (a1, f1, f3, v1, y1)):
        vy = dot(f[...], a[0:128, 256:])
        v[0:128, :] = vy[0:128]
        y[0:128, :] = vy[128:]
        vy = dot(h[...], a[128:256, 256:] - dot(a[0:128, 0:128], vy[128:], 0, 0))
        v[128:256, :] = vy[0:128]
        y[128:256, :] = vy[128:]

    p0 = dot(v0[:, 256:512], y0[...], 0, 0)
    p1 = dot(v1[:, 0:256], y1[...], 0, 0)
    a2[:, 0:256] = g[0, 4] + g[1, 4] - p0[:, 256:512] - p1[:, 0:256]
    a2[:, 256:512] = -p0[:, 0:256]
    a2[:, 512:768] = -p1[:, 256:512]
    solve(a2, f0, v2, y2)

    start = pl.multiple_of(tile // 2 * 128, 128)
    cols = pl.multiple_of(col * 256, 256)
    a0[:, 0:128] = v2[:, pl.ds(start, 128)]
    a0[:, 128:256] = v2[:, pl.ds(start + 256, 128)]
    a0[:, 256:512] = y2[:, pl.ds(cols, 256)]
    a1[:, 0:128] = jnp.where(col == 0, v0[:, pl.ds(start, 128)], v1[:, pl.ds(start + 256, 128)])
    a1[:, 256:512] = jnp.where(col == 0, y0[:, 0:256], y1[:, 256:512])
    a2[:, 0:256] = dot(a0[:, 0:256], a0[:, 256:512], 0, 0)
    a2[0:128, 256:512] = dot(a1[:, 0:128], a1[:, 256:512], 0, 0)
    row = pl.multiple_of(core * 64, 64)
    wait1(5)
    own = g[col, 5, pl.ds(pl.multiple_of(tile * 64, 64), 64), :] - a2[pl.ds(row, 64), 256:512]
    ob[0:64, :] = jnp.where(col == 0, own, 0.0) - a2[pl.ds(row, 64), 0:256]
    ob[64:128, :] = jnp.where(col == 1, own, 0.0) - a2[pl.ds(128 + row, 64), 0:256]

    def result(to):
        return ob.at[pl.ds(pl.multiple_of(to * 32, 32), 32), :]

    outs = [remote(result((b + d) % 4), out_ref.at[b], sendo.at[d - 1], recvo.at[d - 1], line[d]) for d in (1, 2, 3)]
    for c in outs:
        c.start()
    home = pltpu.make_async_copy(result(b), out_ref.at[b], recvo.at[3])
    home.start()
    for c in outs:
        c.wait_send()
    for d in (1, 2, 3):
        p = out_ref.at[(b + 4 - d) % 4]
        pltpu.make_async_copy(p, p, recvo.at[d - 1]).wait()
    home.wait()
    for c in started:
        c.wait_send()

    @pl.when(is_s)
    def _():
        for c in first(0, col, b // 2)[0]:
            c.wait_send()

    @pl.when(jnp.logical_not(is_s))
    def _():
        for kind, face, slot in ((0, 1 - col, 2 + b // 2), (1, col, own_slot)):
            for c in first(kind, face, slot)[0]:
                c.wait_send()


def per_device(box_operators):
    V = pltpu.VMEM
    f = jnp.float32
    dma = pltpu.SemaphoreType.DMA
    out = pl.pallas_call(
        kernel,
        out_shape=jax.ShapeDtypeStruct((4, 32, 256), f),
        in_specs=[pl.BlockSpec(memory_space=pl.ANY)],
        out_specs=pl.BlockSpec(memory_space=pl.ANY),
        scratch_shapes=[V((2, 6, 256, 256), f), V((128, 256), f)] + [V((256, 768), f)] * 3 + [V((256, 512), f)] * 6
        + [V((256, 128), f)] * 4
        + [dma((2, 3)), dma((6,)), dma((9, SLOTS)), dma((9, SLOTS)), dma((3,)), dma((4,))],
        compiler_params=pltpu.CompilerParams(vmem_limit_bytes=40 << 20, collective_id=0, has_side_effects=True),
    )(box_operators[:, 0])
    return out[:, None]


def solution(mesh):
    return jax.shard_map(
        per_device,
        mesh=mesh,
        in_specs=(P(None, "box", None, "tile", "col"),),
        out_specs=P(None, "box", "tile", "col"),
        check_vma=False,
    )
```

```python
import jax
import jax.numpy as jnp
from jax import lax
from jax.experimental import pallas as pl
from jax.experimental.pallas import tpu as pltpu
from jax.sharding import PartitionSpec as P

HI = lax.Precision.HIGHEST

def dot(a, b, ca=1, cb=0):
    return lax.dot_general(a, b, (((ca,), (cb,)), ((), ())), precision=HI, preferred_element_type=jnp.float32)

def leaf(cols, sub):
    cols = list(cols)
    for k in range(8):
        piv = 1.0 / jnp.broadcast_to(cols[k][k:k+1, :], (8, 128))
        here = sub == k
        ck = cols[k]
        for c in range(8):
            if c == k:
                continue
            row = jnp.broadcast_to(cols[c][k:k+1, :], (8, 128)) * piv
            cols[c] = jnp.where(here, row, cols[c] - ck * row)
        cols[k] = jnp.where(here, piv, -ck * piv)
    return cols

def treesum(xs):
    while len(xs) > 1:
        xs = [xs[i] + xs[i+1] if i + 1 < len(xs) else xs[i] for i in range(0, len(xs), 2)]
    return xs[0]

def apply8(cols, y):
    return treesum([cols[j] * jnp.broadcast_to(y[j:j+1, :], (8, 128)) for j in range(8)])

def eliminate(mats, hook=None):
    sub = lax.broadcasted_iota(jnp.int32, (8, 128), 0)
    lane = lax.broadcasted_iota(jnp.int32, (8, 128), 1)
    mats = [list(m) for m in mats]
    es = [[] for _ in mats]
    des = [[] for _ in mats]
    for k in range(16):
        if hook is not None:
            hook(k)
        lo = 8 * k
        inblk = (lane >= lo) & (lane < lo + 8)
        eye = jnp.where(lane == sub + lo, 1.0, 0.0).astype(jnp.float32)
        for n, m in enumerate(mats):
            r = m[k]
            cols = leaf([jnp.broadcast_to(r[:, lo+c:lo+c+1], (8, 128)) for c in range(8)], sub)
            rm = jnp.where(inblk, eye, r)
            y = apply8(cols, rm)
            es[n].append(jnp.where(lane < lo + 8, rm, 0.0))
            des[n].append(jnp.where(lane < lo + 8, y, 0.0))
            ys = [jnp.broadcast_to(y[j:j+1, :], (8, 128)) for j in range(8)]
            for i in range(k + 1, 16):
                a = m[i]
                upd = treesum([jnp.broadcast_to(a[:, lo+j:lo+j+1], (8, 128)) * ys[j] for j in range(8)])
                m[i] = jnp.where(inblk, 0.0, a) - upd
    return es, des

def factor(mat_refs, fac_refs, hook=None):
    es, des = eliminate([[m[8*i:8*i+8, :] for i in range(16)] for m in mat_refs], hook)
    for f, e, d in zip(fac_refs, es, des):
        for i in range(16):
            f[8*i:8*i+8, :] = e[i]
            f[128+8*i:128+8*i+8, :] = d[i]

def solve(a, fac, v, y):
    factor([a.at[0:128, 0:128]], [fac])
    vy = dot(fac[...], a[0:128, 128:])
    v[0:128, :] = vy[0:128, 128:]
    y[0:128, :] = vy[128:, 128:]
    a[128:256, 128:] = a[128:256, 128:] - dot(vy[0:128, 0:128], vy[128:, :], 0, 0)
    factor([a.at[128:256, 128:256]], [fac])
    vy = dot(fac[...], a[128:256, 256:])
    v[128:256, :] = vy[0:128, :]
    y[128:256, :] = vy[128:, :]


MESH = pl.DeviceIdType.MESH

def kernel(x_ref, out_ref, g, ob, a0, a1, a2, v0, v1, v2, y0, y1, y2, f0, f1, f2, f3,
           send1, recv1, send2, recv2, sendo, recvo):
    box = lax.axis_index("box")
    tile = lax.axis_index("tile")
    col = lax.axis_index("col")
    b = box % 4
    quad = box - b
    core = tile % 2
    x = 2 * col + tile // 2

    def at(dz, dx):
        xx = (x + dx) % 4
        return {"box": quad + (b + dz) % 4, "col": xx // 2, "tile": xx % 2 * 2 + core}

    sib = {"tile": tile + 1 - 2 * core}

    barrier = pltpu.get_barrier_semaphore()
    for dev in [at(d, 0) for d in (1, 2, 3)] + [at(0, d) for d in (1, 2, 3)] + [sib]:
        pl.semaphore_signal(barrier, inc=1, device_id=dev, device_id_type=MESH)
    pl.semaphore_wait(barrier, 7)

    def remote(src, dst, s, r, dev):
        return pltpu.make_async_remote_copy(src_ref=src, dst_ref=dst, send_sem=s, recv_sem=r,
                                            device_id=dev, device_id_type=MESH)

    def wait_for(p, sem):
        pltpu.make_async_copy(p, p, sem).wait()

    def rows_of(t):
        return pl.ds(pl.multiple_of(t * 64, 64), 64)

    rows = rows_of(tile)
    LO, HI_, ALL = pl.ds(0, 128), pl.ds(128, 128), pl.ds(0, 256)

    is_s = col != b % 2
    is_w = jnp.logical_not(is_s)
    is_top = tile // 2 == 0
    is_bottom = tile // 2 == 1
    own_slot = jnp.where((b == 1) | (b == 2), 4, 5)

    def first(kind, face, slot, cs, sem):
        dst = g.at[col, slot, rows, cs]
        away = [remote(x_ref.at[(b + d) % 4, face, :, cs], dst, send1.at[kind, d - 1], recv1.at[sem], at(d, 0))
                for d in (1, 3, 2)]
        return away, lambda: pltpu.make_async_copy(x_ref.at[b, face, :, cs], dst, recv1.at[sem])

    def first_a():
        return first(0, col, b // 2, LO, 6 + b // 2)

    def first_b():
        return first(1, col, b // 2, HI_, b // 2)

    def first_w():
        return first(0, 1 - col, 2 + b // 2, ALL, 2 + b // 2)

    def first_own():
        return first(1, col, own_slot, ALL, own_slot)

    def begin(cond, *makers):
        @pl.when(cond)
        def _():
            for maker in makers:
                away, home = maker()
                for c in away:
                    c.start()
                home().start()

    def sent(cond, *makers):
        @pl.when(cond)
        def _():
            for maker in makers:
                for c in maker()[0]:
                    c.wait_send()

    A, B, W = range(3)
    SLOTS = (pl.ds(0, 2), pl.ds(0, 2), pl.ds(2, 3))
    CS = (LO, HI_, ALL)
    SEMS = (((0, 6), (1, 7)), ((0, 0), (1, 1)), ((2, 2), (3, 3), (4, 4)))
    pending = []

    def under(cond, fn):
        if cond is None:
            fn()
        else:
            pl.when(cond)(fn)

    def piece(unit, d, other=0):
        xx = (x + d) % 4
        t = xx % 2 * 2 + core + other * (1 - 2 * core)
        return g.at[xx // 2, SLOTS[unit], rows_of(t), CS[unit]]

    def ring_copy(unit, src, n):
        p = piece(unit, src)
        return remote(p, p, send2.at[unit, n], recv2.at[unit, n], at(0, n) if n in (1, 2, 3) else sib)

    def go(cond, *args):
        ring_copy(*args).start()
        pending.append((cond, args))

    def have(unit, d):
        return None if unit != A else is_top if d % 2 == 0 else is_bottom

    def ring_start(unit):
        cond = have(unit, 0)

        def do():
            for slot, sem in SEMS[unit]:
                wait_for(g.at[col, slot, rows, CS[unit]], recv1.at[sem])
            for d in (2, 1, 3):
                go(cond, unit, 0, d)
            go(cond, unit, 0, 0)
        under(cond, do)

    def ring_share(unit):
        for d in (1, 3, 2):
            cond = have(unit, d)

            def do():
                wait_for(piece(unit, 4 - d), recv2.at[unit, d])
                go(cond, unit, 4 - d, 3 + d)
            under(cond, do)

    def ring_done(unit):
        under(have(unit, 0), lambda: wait_for(piece(unit, 0, 1), recv2.at[unit, 0]))
        for d in (1, 3, 2):
            under(have(unit, d), lambda: wait_for(piece(unit, 4 - d, 1), recv2.at[unit, 3 + d]))

    begin(is_s & is_top, first_a)
    begin(is_s, first_b)
    begin(is_w & is_bottom, first_w, first_own)
    ring_start(A)
    begin(is_w & is_top, first_w, first_own)
    ring_share(A)
    ring_start(B)
    ring_done(A)

    during_first = {3: lambda: ring_start(W), 11: lambda: ring_share(B)}
    during_second = {12: lambda: ring_share(W)}

    def hook(table):
        return lambda k: table[k]() if k in table else None

    for p, a in enumerate((a0, a1)):
        a[0:128, 0:128] = g[0, p, 0:128, 0:128] + g[1, p, 0:128, 0:128]
    factor([a.at[0:128, 0:128] for a in (a0, a1)], [f0, f1], hook(during_first))
    ring_done(B)
    for p, (a, f) in enumerate(((a0, f0), (a1, f1))):
        vy = dot(f[...], g[0, p, 0:128, 128:256] + g[1, p, 0:128, 128:256])
        a[0:128, 0:128] = vy[0:128]
        a[128:256, 128:256] = g[0, p, 128:256, 128:256] + g[1, p, 128:256, 128:256] - dot(vy[0:128], vy[128:], 0, 0)
    factor([a.at[128:256, 128:256] for a in (a0, a1)], [f2, f3], hook(during_second))
    ring_done(W)
    for p, a in enumerate((a0, a1)):
        a[:, 256:512] = g[0, 2 + p]
        a[:, 512:768] = g[1, 2 + p]
    for a, f, h, v, y in ((a0, f0, f2, v0, y0), (a1, f1, f3, v1, y1)):
        vy = dot(f[...], a[0:128, 256:])
        v[0:128, :] = vy[0:128]
        y[0:128, :] = vy[128:]
        vy = dot(h[...], a[128:256, 256:] - dot(a[0:128, 0:128], vy[128:], 0, 0))
        v[128:256, :] = vy[0:128]
        y[128:256, :] = vy[128:]

    p0 = dot(v0[:, 256:512], y0[...], 0, 0)
    p1 = dot(v1[:, 0:256], y1[...], 0, 0)
    a2[:, 0:256] = g[0, 4] + g[1, 4] - p0[:, 256:512] - p1[:, 0:256]
    a2[:, 256:512] = -p0[:, 0:256]
    a2[:, 512:768] = -p1[:, 256:512]
    solve(a2, f0, v2, y2)

    start = pl.multiple_of(tile // 2 * 128, 128)
    cols = pl.multiple_of(col * 256, 256)
    a0[:, 0:128] = v2[:, pl.ds(start, 128)]
    a0[:, 128:256] = v2[:, pl.ds(start + 256, 128)]
    a0[:, 256:512] = y2[:, pl.ds(cols, 256)]
    a1[:, 0:128] = jnp.where(col == 0, v0[:, pl.ds(start, 128)], v1[:, pl.ds(start + 256, 128)])
    a1[:, 256:512] = jnp.where(col == 0, y0[:, 0:256], y1[:, 256:512])
    a2[:, 0:256] = dot(a0[:, 0:256], a0[:, 256:512], 0, 0)
    a2[0:128, 256:512] = dot(a1[:, 0:128], a1[:, 256:512], 0, 0)
    row = pl.multiple_of(core * 64, 64)
    wait_for(g.at[col, 5, rows, :], recv1.at[5])
    own = g[col, 5, rows, :] - a2[pl.ds(row, 64), 256:512]
    ob[0:64, :] = jnp.where(col == 0, own, 0.0) - a2[pl.ds(row, 64), 0:256]
    ob[64:128, :] = jnp.where(col == 1, own, 0.0) - a2[pl.ds(128 + row, 64), 0:256]

    def result(to):
        return ob.at[pl.ds(pl.multiple_of(to * 32, 32), 32), :]

    outs = [remote(result((b + d) % 4), out_ref.at[b], sendo.at[d - 1], recvo.at[d - 1], at(d, 0)) for d in (1, 2, 3)]
    for c in outs:
        c.start()
    home = pltpu.make_async_copy(result(b), out_ref.at[b], recvo.at[3])
    home.start()
    for c in outs:
        c.wait_send()
    for d in (1, 2, 3):
        wait_for(out_ref.at[(b + 4 - d) % 4], recvo.at[d - 1])
    home.wait()
    for cond in (None, is_top, is_bottom):
        def drain():
            for c, args in pending:
                if c is cond:
                    ring_copy(*args).wait_send()
        under(cond, drain)
    sent(is_s & is_top, first_a)
    sent(is_s, first_b)
    sent(is_w, first_w, first_own)


def per_device(box_operators):
    V = pltpu.VMEM
    f = jnp.float32
    dma = pltpu.SemaphoreType.DMA
    out = pl.pallas_call(
        kernel,
        out_shape=jax.ShapeDtypeStruct((4, 32, 256), f),
        in_specs=[pl.BlockSpec(memory_space=pl.ANY)],
        out_specs=pl.BlockSpec(memory_space=pl.ANY),
        scratch_shapes=[V((2, 6, 256, 256), f), V((128, 256), f)] + [V((256, 768), f)] * 3 + [V((256, 512), f)] * 6
        + [V((256, 128), f)] * 4
        + [dma((2, 3)), dma((8,)), dma((3, 7)), dma((3, 7)), dma((3,)), dma((4,))],
        compiler_params=pltpu.CompilerParams(vmem_limit_bytes=40 << 20, collective_id=0, has_side_effects=True),
    )(box_operators[:, 0])
    return out[:, None]


def solution(mesh):
    return jax.shard_map(
        per_device,
        mesh=mesh,
        in_specs=(P(None, "box", None, "tile", "col"),),
        out_specs=P(None, "box", "tile", "col"),
        check_vma=False,
    )
```

```python
import jax
import jax.numpy as jnp
from jax import lax
from jax.experimental import pallas as pl
from jax.experimental.pallas import tpu as pltpu
from jax.sharding import PartitionSpec as P

HI = lax.Precision.HIGHEST

def dot(a, b, ca=1, cb=0):
    return lax.dot_general(a, b, (((ca,), (cb,)), ((), ())), precision=HI, preferred_element_type=jnp.float32)

def leaf(cols, sub):
    cols = list(cols)
    scale = None
    for k in range(8):
        piv = 1.0 / jnp.broadcast_to(cols[k][k:k + 1, :], (8, 128))
        here = sub == k
        factors = jnp.where(here, 0.0, cols[k]) * piv
        scale = piv if scale is None else jnp.where(sub >= k, piv, scale)
        for q in range(1, 8):
            c = (k + q) % 8
            cols[c] = cols[c] - factors * jnp.broadcast_to(cols[c][k:k + 1, :], (8, 128))
        cols[k] = jnp.where(here, 1.0, -factors)
    return [c * scale for c in cols]


def treesum(xs):
    while len(xs) > 1:
        xs = [xs[i] + xs[i+1] if i + 1 < len(xs) else xs[i] for i in range(0, len(xs), 2)]
    return xs[0]

def apply8(cols, y):
    return treesum([cols[j] * jnp.broadcast_to(y[j:j+1, :], (8, 128)) for j in range(8)])

PANEL = 4
LOOK = 2


def eliminate(mats, hook=None):
    sub = lax.broadcasted_iota(jnp.int32, (8, 128), 0)
    lane = lax.broadcasted_iota(jnp.int32, (8, 128), 1)
    mats = [list(m) for m in mats]
    es = [[] for _ in mats]
    fs = [[] for _ in mats]
    panels = [[] for _ in mats]
    for k in range(16):
        if hook is not None:
            hook(k)
        lo = 8 * k
        end = k // PANEL * PANEL + PANEL
        inside = (lane >= lo) & (lane < lo + 8)
        eye = jnp.where(lane == sub + lo, 1.0, 0.0).astype(jnp.float32)
        for n, m in enumerate(mats):
            r = m[k]
            cols = leaf([jnp.broadcast_to(r[:, lo + c:lo + c + 1], (8, 128)) for c in range(8)], sub)
            rm = jnp.where(inside, eye, r)
            y = apply8(cols, rm)
            es[n].append(jnp.where(lane < lo + 8, rm, 0.0))
            fs[n].append(jnp.where(lane < lo + 8, y, 0.0))
            panels[n].append((rm, jnp.where((lane >= lo + 8) & (lane < 8 * end), 0.0, y)))
            yb = [jnp.broadcast_to(y[j:j + 1, :], (8, 128)) for j in range(8)]
            for i in range(k + 1, min(end + LOOK, 16)):
                a = m[i]
                m[i] = jnp.where(inside, 0.0, a) - treesum(
                    [jnp.broadcast_to(a[:, lo + j:lo + j + 1], (8, 128)) * yb[j] for j in range(8)])
        if k + 1 == end and end + LOOK < 16:
            gone = (lane >= 8 * (end - PANEL)) & (lane < 8 * end)
            for n, m in enumerate(mats):
                v = jnp.concatenate([p[0] for p in panels[n]], axis=0)
                y = jnp.concatenate([p[1] for p in panels[n]], axis=0)
                update = dot(v, y, 0, 0)
                for i in range(end + LOOK, 16):
                    m[i] = jnp.where(gone, 0.0, m[i]) - update[8 * i:8 * i + 8, :]
        if k + 1 == end:
            panels = [[] for _ in mats]
    return es, fs


def factor(mat_refs, fac_refs, hook=None):
    es, des = eliminate([[m[8*i:8*i+8, :] for i in range(16)] for m in mat_refs], hook)
    for f, e, d in zip(fac_refs, es, des):
        for i in range(16):
            f[8*i:8*i+8, :] = e[i]
            f[128+8*i:128+8*i+8, :] = d[i]

def dot3(a, b, ca=1, cb=0):
    ah = a.astype(jnp.bfloat16)
    al = (a - ah.astype(jnp.float32)).astype(jnp.bfloat16)
    bh = b.astype(jnp.bfloat16)
    bl = (b - bh.astype(jnp.float32)).astype(jnp.bfloat16)

    def one(p, q):
        return lax.dot_general(p, q, (((ca,), (cb,)), ((), ())), preferred_element_type=jnp.float32)
    return one(ah, bh) + (one(ah, bl) + one(al, bh))


def solve(a, fac, v, y):
    factor([a.at[0:128, 0:128]], [fac])
    vy = dot(fac[...], a[0:128, 128:])
    v[0:128, :] = vy[0:128, 128:]
    y[0:128, :] = vy[128:, 128:]
    a[128:256, 128:] = a[128:256, 128:] - dot(vy[0:128, 0:128], vy[128:, :], 0, 0)
    factor([a.at[128:256, 128:256]], [fac])
    vy = dot(fac[...], a[128:256, 256:])
    v[128:256, :] = vy[0:128, :]
    y[128:256, :] = vy[128:, :]


MESH = pl.DeviceIdType.MESH

def kernel(x_ref, out_ref, g, ob, a0, a1, a2, v0, v1, v2, y0, y1, y2, f0, f1, f2, f3,
           send1, recv1, send2, recv2, sendo, recvo):
    box = lax.axis_index("box")
    tile = lax.axis_index("tile")
    col = lax.axis_index("col")
    b = box % 4
    quad = box - b
    core = tile % 2
    x = 2 * col + tile // 2

    def at(dz, dx):
        xx = (x + dx) % 4
        return {"box": quad + (b + dz) % 4, "col": xx // 2, "tile": xx % 2 * 2 + core}

    sib = {"tile": tile + 1 - 2 * core}

    barrier = pltpu.get_barrier_semaphore()
    for dev in [at(d, 0) for d in (1, 2, 3)] + [at(0, d) for d in (1, 2, 3)] + [sib]:
        pl.semaphore_signal(barrier, inc=1, device_id=dev, device_id_type=MESH)
    pl.semaphore_wait(barrier, 7)

    def remote(src, dst, s, r, dev):
        return pltpu.make_async_remote_copy(src_ref=src, dst_ref=dst, send_sem=s, recv_sem=r,
                                            device_id=dev, device_id_type=MESH)

    def wait_for(p, sem):
        pltpu.make_async_copy(p, p, sem).wait()

    def rows_of(t):
        return pl.ds(pl.multiple_of(t * 64, 64), 64)

    rows = rows_of(tile)
    LO, HI_, ALL = pl.ds(0, 128), pl.ds(128, 128), pl.ds(0, 256)

    is_s = col != b % 2
    is_w = jnp.logical_not(is_s)
    is_top = tile // 2 == 0
    is_bottom = tile // 2 == 1
    own_slot = jnp.where((b == 1) | (b == 2), 4, 5)

    def first(kind, face, slot, cs, sem):
        dst = g.at[col, slot, rows, cs]
        away = [remote(x_ref.at[(b + d) % 4, face, :, cs], dst, send1.at[kind, d - 1], recv1.at[sem], at(d, 0))
                for d in (1, 3, 2)]
        return away, lambda: pltpu.make_async_copy(x_ref.at[b, face, :, cs], dst, recv1.at[sem])

    def first_a():
        return first(0, col, b // 2, LO, 6 + b // 2)

    def first_b():
        return first(1, col, b // 2, HI_, b // 2)

    def first_w():
        return first(0, 1 - col, 2 + b // 2, ALL, 2 + b // 2)

    def first_own():
        return first(1, col, own_slot, ALL, own_slot)

    def begin(cond, *makers):
        @pl.when(cond)
        def _():
            for maker in makers:
                away, home = maker()
                for c in away:
                    c.start()
                home().start()

    def sent(cond, *makers):
        @pl.when(cond)
        def _():
            for maker in makers:
                for c in maker()[0]:
                    c.wait_send()

    A, B, W = range(3)
    SLOTS = (pl.ds(0, 2), pl.ds(0, 2), pl.ds(2, 3))
    CS = (LO, HI_, ALL)
    SEMS = (((0, 6), (1, 7)), ((0, 0), (1, 1)), ((2, 2), (3, 3), (4, 4)))
    pending = []

    def under(cond, fn):
        if cond is None:
            fn()
        else:
            pl.when(cond)(fn)

    def piece(unit, d, other=0):
        xx = (x + d) % 4
        t = xx % 2 * 2 + core + other * (1 - 2 * core)
        return g.at[xx // 2, SLOTS[unit], rows_of(t), CS[unit]]

    def ring_copy(unit, src, n):
        p = piece(unit, src)
        return remote(p, p, send2.at[unit, n], recv2.at[unit, n], at(0, n) if n in (1, 2, 3) else sib)

    def go(cond, *args):
        ring_copy(*args).start()
        pending.append((cond, args))

    def have(unit, d):
        return None if unit != A else is_top if d % 2 == 0 else is_bottom

    def ring_start(unit):
        cond = have(unit, 0)

        def do():
            for slot, sem in SEMS[unit]:
                wait_for(g.at[col, slot, rows, CS[unit]], recv1.at[sem])
            for d in (2, 1, 3):
                go(cond, unit, 0, d)
            go(cond, unit, 0, 0)
        under(cond, do)

    def ring_share(unit):
        for d in (1, 3, 2):
            cond = have(unit, d)

            def do():
                wait_for(piece(unit, 4 - d), recv2.at[unit, d])
                go(cond, unit, 4 - d, 3 + d)
            under(cond, do)

    def ring_done(unit):
        under(have(unit, 0), lambda: wait_for(piece(unit, 0, 1), recv2.at[unit, 0]))
        for d in (1, 3, 2):
            under(have(unit, d), lambda: wait_for(piece(unit, 4 - d, 1), recv2.at[unit, 3 + d]))

    begin(is_s & is_top, first_a)
    begin(is_s, first_b)
    begin(is_w & is_bottom, first_w, first_own)
    ring_start(A)
    begin(is_w & is_top, first_w, first_own)
    ring_share(A)
    ring_start(B)
    ring_done(A)
    ring_start(W)

    during_first = {}
    during_second = {}

    def hook(table):
        return lambda k: table[k]() if k in table else None

    for p, a in enumerate((a0, a1)):
        a[0:128, 0:128] = g[0, p, 0:128, 0:128] + g[1, p, 0:128, 0:128]
    factor([a.at[0:128, 0:128] for a in (a0, a1)], [f0, f1], hook(during_first))
    ring_share(B)
    ring_done(B)
    for p, (a, f) in enumerate(((a0, f0), (a1, f1))):
        vy = dot(f[...], g[0, p, 0:128, 128:256] + g[1, p, 0:128, 128:256])
        a[0:128, 0:128] = vy[0:128]
        a[128:256, 128:256] = g[0, p, 128:256, 128:256] + g[1, p, 128:256, 128:256] - dot(vy[0:128], vy[128:], 0, 0)
    factor([a.at[128:256, 128:256] for a in (a0, a1)], [f2, f3], hook(during_second))
    ring_share(W)
    ring_done(W)
    for p, a in enumerate((a0, a1)):
        a[:, 256:512] = g[0, 2 + p]
        a[:, 512:768] = g[1, 2 + p]
    for a, f, h, v, y in ((a0, f0, f2, v0, y0), (a1, f1, f3, v1, y1)):
        vy = dot3(f[...], a[0:128, 256:])
        v[0:128, :] = vy[0:128]
        y[0:128, :] = vy[128:]
        vy = dot3(h[...], a[128:256, 256:] - dot3(a[0:128, 0:128], vy[128:], 0, 0))
        v[128:256, :] = vy[0:128]
        y[128:256, :] = vy[128:]

    p0 = dot3(v0[:, 256:512], y0[...], 0, 0)
    p1 = dot3(v1[:, 0:256], y1[...], 0, 0)
    a2[:, 0:256] = g[0, 4] + g[1, 4] - p0[:, 256:512] - p1[:, 0:256]
    a2[:, 256:512] = -p0[:, 0:256]
    a2[:, 512:768] = -p1[:, 256:512]
    solve(a2, f0, v2, y2)

    start = pl.multiple_of(tile // 2 * 128, 128)
    cols = pl.multiple_of(col * 256, 256)
    a0[:, 0:128] = v2[:, pl.ds(start, 128)]
    a0[:, 128:256] = v2[:, pl.ds(start + 256, 128)]
    a0[:, 256:512] = y2[:, pl.ds(cols, 256)]
    a1[:, 0:128] = jnp.where(col == 0, v0[:, pl.ds(start, 128)], v1[:, pl.ds(start + 256, 128)])
    a1[:, 256:512] = jnp.where(col == 0, y0[:, 0:256], y1[:, 256:512])
    a2[:, 0:256] = dot3(a0[:, 0:256], a0[:, 256:512], 0, 0)
    a2[0:128, 256:512] = dot3(a1[:, 0:128], a1[:, 256:512], 0, 0)
    row = pl.multiple_of(core * 64, 64)
    wait_for(g.at[col, 5, rows, :], recv1.at[5])
    own = g[col, 5, rows, :] - a2[pl.ds(row, 64), 256:512]
    ob[0:64, :] = jnp.where(col == 0, own, 0.0) - a2[pl.ds(row, 64), 0:256]
    ob[64:128, :] = jnp.where(col == 1, own, 0.0) - a2[pl.ds(128 + row, 64), 0:256]

    def result(to):
        return ob.at[pl.ds(pl.multiple_of(to * 32, 32), 32), :]

    outs = [remote(result((b + d) % 4), out_ref.at[b], sendo.at[d - 1], recvo.at[d - 1], at(d, 0)) for d in (1, 2, 3)]
    for c in outs:
        c.start()
    home = pltpu.make_async_copy(result(b), out_ref.at[b], recvo.at[3])
    home.start()
    for c in outs:
        c.wait_send()
    for d in (1, 2, 3):
        wait_for(out_ref.at[(b + 4 - d) % 4], recvo.at[d - 1])
    home.wait()
    for cond in (None, is_top, is_bottom):
        def drain():
            for c, args in pending:
                if c is cond:
                    ring_copy(*args).wait_send()
        under(cond, drain)
    sent(is_s & is_top, first_a)
    sent(is_s, first_b)
    sent(is_w, first_w, first_own)


def per_device(box_operators):
    V = pltpu.VMEM
    f = jnp.float32
    dma = pltpu.SemaphoreType.DMA
    out = pl.pallas_call(
        kernel,
        out_shape=jax.ShapeDtypeStruct((4, 32, 256), f),
        in_specs=[pl.BlockSpec(memory_space=pl.ANY)],
        out_specs=pl.BlockSpec(memory_space=pl.ANY),
        scratch_shapes=[V((2, 6, 256, 256), f), V((128, 256), f)] + [V((256, 768), f)] * 3 + [V((256, 512), f)] * 6
        + [V((256, 128), f)] * 4
        + [dma((2, 3)), dma((8,)), dma((3, 7)), dma((3, 7)), dma((3,)), dma((4,))],
        compiler_params=pltpu.CompilerParams(vmem_limit_bytes=40 << 20, collective_id=0, has_side_effects=True),
    )(box_operators[:, 0])
    return out[:, None]


def solution(mesh):
    return jax.shard_map(
        per_device,
        mesh=mesh,
        in_specs=(P(None, "box", None, "tile", "col"),),
        out_specs=P(None, "box", "tile", "col"),
        check_vma=False,
    )
```

```python
import jax
import jax.numpy as jnp
from jax import lax
from jax.experimental import pallas as pl
from jax.experimental.pallas import tpu as pltpu
from jax.sharding import PartitionSpec as P

HI = lax.Precision.HIGHEST

def dot(a, b, ca=1, cb=0):
    return lax.dot_general(a, b, (((ca,), (cb,)), ((), ())), precision=HI, preferred_element_type=jnp.float32)

def leaf(cols, sub):
    cols = list(cols)
    scale = None
    for k in range(8):
        piv = 1.0 / jnp.broadcast_to(cols[k][k:k + 1, :], (8, 128))
        here = sub == k
        factors = jnp.where(here, 0.0, cols[k]) * piv
        scale = piv if scale is None else jnp.where(sub >= k, piv, scale)
        for q in range(1, 8):
            c = (k + q) % 8
            cols[c] = cols[c] - factors * jnp.broadcast_to(cols[c][k:k + 1, :], (8, 128))
        cols[k] = jnp.where(here, 1.0, -factors)
    return [c * scale for c in cols]


def treesum(xs):
    while len(xs) > 1:
        xs = [xs[i] + xs[i+1] if i + 1 < len(xs) else xs[i] for i in range(0, len(xs), 2)]
    return xs[0]

def apply8(cols, y):
    return treesum([cols[j] * jnp.broadcast_to(y[j:j+1, :], (8, 128)) for j in range(8)])

PANEL = 4
LOOK = 2


def eliminate(mats, hook=None):
    sub = lax.broadcasted_iota(jnp.int32, (8, 128), 0)
    lane = lax.broadcasted_iota(jnp.int32, (8, 128), 1)
    mats = [list(m) for m in mats]
    es = [[] for _ in mats]
    fs = [[] for _ in mats]
    panels = [[] for _ in mats]
    for k in range(16):
        if hook is not None:
            hook(k)
        lo = 8 * k
        end = k // PANEL * PANEL + PANEL
        inside = (lane >= lo) & (lane < lo + 8)
        eye = jnp.where(lane == sub + lo, 1.0, 0.0).astype(jnp.float32)
        for n, m in enumerate(mats):
            r = m[k]
            cols = leaf([jnp.broadcast_to(r[:, lo + c:lo + c + 1], (8, 128)) for c in range(8)], sub)
            rm = jnp.where(inside, eye, r)
            y = apply8(cols, rm)
            es[n].append(jnp.where(lane < lo + 8, rm, 0.0))
            fs[n].append(jnp.where(lane < lo + 8, y, 0.0))
            panels[n].append((rm, jnp.where((lane >= lo + 8) & (lane < 8 * end), 0.0, y)))
            yb = [jnp.broadcast_to(y[j:j + 1, :], (8, 128)) for j in range(8)]
            for i in range(k + 1, min(end + LOOK, 16)):
                a = m[i]
                m[i] = jnp.where(inside, 0.0, a) - treesum(
                    [jnp.broadcast_to(a[:, lo + j:lo + j + 1], (8, 128)) * yb[j] for j in range(8)])
        if k + 1 == end and end + LOOK < 16:
            gone = (lane >= 8 * (end - PANEL)) & (lane < 8 * end)
            for n, m in enumerate(mats):
                v = jnp.concatenate([p[0] for p in panels[n]], axis=0)
                y = jnp.concatenate([p[1] for p in panels[n]], axis=0)
                update = dot(v, y, 0, 0)
                for i in range(end + LOOK, 16):
                    m[i] = jnp.where(gone, 0.0, m[i]) - update[8 * i:8 * i + 8, :]
        if k + 1 == end:
            panels = [[] for _ in mats]
    return es, fs


def factor(mat_refs, fac_refs, hook=None):
    es, des = eliminate([[m[8*i:8*i+8, :] for i in range(16)] for m in mat_refs], hook)
    for f, e, d in zip(fac_refs, es, des):
        for i in range(16):
            f[8*i:8*i+8, :] = e[i]
            f[128+8*i:128+8*i+8, :] = d[i]

def dot3(a, b, ca=1, cb=0):
    ah = a.astype(jnp.bfloat16)
    al = (a - ah.astype(jnp.float32)).astype(jnp.bfloat16)
    bh = b.astype(jnp.bfloat16)
    bl = (b - bh.astype(jnp.float32)).astype(jnp.bfloat16)

    def one(p, q):
        return lax.dot_general(p, q, (((ca,), (cb,)), ((), ())), preferred_element_type=jnp.float32)
    return one(ah, bh) + (one(ah, bl) + one(al, bh))


def solve(a, fac, fac2, v, y):
    factor([a.at[0:128, 0:128]], [fac])
    vy = dot(fac[...], a[0:128, 128:256])
    a[128:256, 128:256] = a[128:256, 128:256] - dot(vy[0:128], vy[128:], 0, 0)
    wide = dot3(fac[...], a[0:128, 256:])
    v[0:128, :] = wide[0:128]
    y[0:128, :] = wide[128:]
    a[128:256, 256:] = a[128:256, 256:] - dot3(vy[0:128], wide[128:], 0, 0)
    factor([a.at[128:256, 128:256]], [fac2])
    wide = dot3(fac2[...], a[128:256, 256:])
    v[128:256, :] = wide[0:128]
    y[128:256, :] = wide[128:]


MESH = pl.DeviceIdType.MESH

def kernel(x_ref, out_ref, g, ob, a0, a1, a2, v0, v1, v2, y0, y1, y2, f0, f1, f2, f3, e0, e1,
           send1, recv1, send2, recv2, sendo, recvo):
    box = lax.axis_index("box")
    tile = lax.axis_index("tile")
    col = lax.axis_index("col")
    b = box % 4
    quad = box - b
    core = tile % 2
    x = 2 * col + tile // 2

    def at(dz, dx):
        xx = (x + dx) % 4
        return {"box": quad + (b + dz) % 4, "col": xx // 2, "tile": xx % 2 * 2 + core}

    sib = {"tile": tile + 1 - 2 * core}

    barrier = pltpu.get_barrier_semaphore()
    for dev in [at(d, 0) for d in (1, 2, 3)] + [at(0, d) for d in (1, 2, 3)] + [sib]:
        pl.semaphore_signal(barrier, inc=1, device_id=dev, device_id_type=MESH)
    pl.semaphore_wait(barrier, 7)

    def remote(src, dst, s, r, dev):
        return pltpu.make_async_remote_copy(src_ref=src, dst_ref=dst, send_sem=s, recv_sem=r,
                                            device_id=dev, device_id_type=MESH)

    def wait_for(p, sem):
        pltpu.make_async_copy(p, p, sem).wait()

    def rows_of(t):
        return pl.ds(pl.multiple_of(t * 64, 64), 64)

    rows = rows_of(tile)
    LO, HI_, ALL = pl.ds(0, 128), pl.ds(128, 128), pl.ds(0, 256)

    is_s = col != b % 2
    is_w = jnp.logical_not(is_s)
    is_top = tile // 2 == 0
    is_bottom = tile // 2 == 1
    own_slot = jnp.where((b == 1) | (b == 2), 4, 5)

    def first(kind, face, slot, cs, sem):
        dst = g.at[col, slot, rows, cs]
        away = [remote(x_ref.at[(b + d) % 4, face, :, cs], dst, send1.at[kind, d - 1], recv1.at[sem], at(d, 0))
                for d in (1, 3, 2)]
        return away, lambda: pltpu.make_async_copy(x_ref.at[b, face, :, cs], dst, recv1.at[sem])

    def first_a():
        return first(0, col, b // 2, LO, 6 + b // 2)

    def first_b():
        return first(1, col, b // 2, HI_, b // 2)

    def first_w():
        return first(0, 1 - col, 2 + b // 2, ALL, 2 + b // 2)

    def first_own():
        return first(1, col, own_slot, ALL, own_slot)

    def begin(cond, *makers):
        @pl.when(cond)
        def _():
            for maker in makers:
                away, home = maker()
                for c in away:
                    c.start()
                home().start()

    def sent(cond, *makers):
        @pl.when(cond)
        def _():
            for maker in makers:
                for c in maker()[0]:
                    c.wait_send()

    A, B, W = range(3)
    SLOTS = (pl.ds(0, 2), pl.ds(0, 2), pl.ds(2, 3))
    CS = (LO, HI_, ALL)
    SEMS = (((0, 6), (1, 7)), ((0, 0), (1, 1)), ((2, 2), (3, 3), (4, 4)))
    pending = []

    def under(cond, fn):
        if cond is None:
            fn()
        else:
            pl.when(cond)(fn)

    def piece(unit, d, other=0):
        xx = (x + d) % 4
        t = xx % 2 * 2 + core + other * (1 - 2 * core)
        return g.at[xx // 2, SLOTS[unit], rows_of(t), CS[unit]]

    def ring_copy(unit, src, n):
        p = piece(unit, src)
        return remote(p, p, send2.at[unit, n], recv2.at[unit, n], at(0, n) if n in (1, 2, 3) else sib)

    def go(cond, *args):
        ring_copy(*args).start()
        pending.append((cond, args))

    def have(unit, d):
        return None if unit != A else is_top if d % 2 == 0 else is_bottom

    def ring_start(unit):
        cond = have(unit, 0)

        def do():
            for slot, sem in SEMS[unit]:
                wait_for(g.at[col, slot, rows, CS[unit]], recv1.at[sem])
            for d in (2, 1, 3):
                go(cond, unit, 0, d)
            go(cond, unit, 0, 0)
        under(cond, do)

    def ring_share(unit, ds=(1, 3, 2)):
        for d in ds:
            cond = have(unit, d)

            def do():
                wait_for(piece(unit, 4 - d), recv2.at[unit, d])
                go(cond, unit, 4 - d, 3 + d)
            under(cond, do)

    def ring_done(unit):
        under(have(unit, 0), lambda: wait_for(piece(unit, 0, 1), recv2.at[unit, 0]))
        for d in (1, 3, 2):
            under(have(unit, d), lambda: wait_for(piece(unit, 4 - d, 1), recv2.at[unit, 3 + d]))

    begin(is_s & is_top, first_a)
    begin(is_s, first_b)
    begin(is_w & is_bottom, first_w, first_own)
    ring_start(A)
    begin(is_w & is_top, first_w, first_own)
    ring_share(A)
    ring_start(B)
    ring_done(A)
    ring_start(W)

    during_first = {}
    during_second = {}

    def hook(table):
        return lambda k: table[k]() if k in table else None

    for p, a in enumerate((a0, a1)):
        a[0:128, 0:128] = g[0, p, 0:128, 0:128] + g[1, p, 0:128, 0:128]
    factor([a.at[0:128, 0:128] for a in (a0, a1)], [f0, f1], hook(during_first))
    ring_share(B)
    ring_done(B)
    for p, (a, f) in enumerate(((a0, f0), (a1, f1))):
        vy = dot(f[...], g[0, p, 0:128, 128:256] + g[1, p, 0:128, 128:256])
        a[0:128, 0:128] = vy[0:128]
        a[128:256, 128:256] = g[0, p, 128:256, 128:256] + g[1, p, 128:256, 128:256] - dot(vy[0:128], vy[128:], 0, 0)
    factor([a.at[128:256, 128:256] for a in (a0, a1)], [f2, f3], hook(during_second))
    ring_share(W)
    for a, f, h, ef in ((a0, f0, f2, e0), (a1, f1, f3, e1)):
        low = dot3(h[...], -dot3(a[0:128, 0:128], f[128:256, :], 0, 0))
        ef[0:128, 0:128] = f[0:128, :]
        ef[0:128, 128:256] = jnp.zeros((128, 128), jnp.float32)
        ef[128:256, 0:128] = low[0:128]
        ef[128:256, 128:256] = h[0:128, :]
        ef[256:384, 0:128] = f[128:256, :]
        ef[256:384, 128:256] = jnp.zeros((128, 128), jnp.float32)
        ef[384:512, 0:128] = low[128:]
        ef[384:512, 128:256] = h[128:256, :]
    ring_done(W)
    for p, (ef, v, y) in enumerate(((e0, v0, y0), (e1, v1, y1))):
        for c in (1 - p, p):
            vy = dot3(ef[...], g[c, 2 + p])
            v[:, 256 * c:256 * c + 256] = vy[0:256]
            y[:, 256 * c:256 * c + 256] = vy[256:512]

    a2[:, 0:256] = (g[0, 4] + g[1, 4] - dot3(v0[:, 256:512], y0[:, 256:512], 0, 0)
                    - dot3(v1[:, 0:256], y1[:, 0:256], 0, 0))
    a2[:, 256:512] = -dot3(v0[:, 256:512], y0[:, 0:256], 0, 0)
    a2[:, 512:768] = -dot3(v1[:, 0:256], y1[:, 256:512], 0, 0)

    start = pl.multiple_of(tile // 2 * 128, 128)
    cols = pl.multiple_of(col * 256, 256)
    a1[:, 0:128] = jnp.where(col == 0, v0[:, pl.ds(start, 128)], v1[:, pl.ds(start + 256, 128)])
    a1[:, 256:512] = jnp.where(col == 0, y0[:, 0:256], y1[:, 256:512])
    a0[0:128, 512:768] = dot3(a1[:, 0:128], a1[:, 256:512], 0, 0)
    solve(a2, f0, f1, v2, y2)

    a0[:, 0:128] = v2[:, pl.ds(start, 128)]
    a0[:, 128:256] = v2[:, pl.ds(start + 256, 128)]
    a0[:, 256:512] = y2[:, pl.ds(cols, 256)]
    a2[:, 0:256] = dot3(a0[:, 0:256], a0[:, 256:512], 0, 0)
    row = pl.multiple_of(core * 64, 64)
    wait_for(g.at[col, 5, rows, :], recv1.at[5])
    own = g[col, 5, rows, :] - a0[pl.ds(row, 64), 512:768]
    ob[0:64, :] = jnp.where(col == 0, own, 0.0) - a2[pl.ds(row, 64), 0:256]
    ob[64:128, :] = jnp.where(col == 1, own, 0.0) - a2[pl.ds(128 + row, 64), 0:256]

    def result(to):
        return ob.at[pl.ds(pl.multiple_of(to * 32, 32), 32), :]

    outs = [remote(result((b + d) % 4), out_ref.at[b], sendo.at[d - 1], recvo.at[d - 1], at(d, 0)) for d in (1, 2, 3)]
    for c in outs:
        c.start()
    home = pltpu.make_async_copy(result(b), out_ref.at[b], recvo.at[3])
    home.start()
    for c in outs:
        c.wait_send()
    for d in (1, 2, 3):
        wait_for(out_ref.at[(b + 4 - d) % 4], recvo.at[d - 1])
    home.wait()
    for cond in (None, is_top, is_bottom):
        def drain():
            for c, args in pending:
                if c is cond:
                    ring_copy(*args).wait_send()
        under(cond, drain)
    sent(is_s & is_top, first_a)
    sent(is_s, first_b)
    sent(is_w, first_w, first_own)


def per_device(box_operators):
    V = pltpu.VMEM
    f = jnp.float32
    dma = pltpu.SemaphoreType.DMA
    out = pl.pallas_call(
        kernel,
        out_shape=jax.ShapeDtypeStruct((4, 32, 256), f),
        in_specs=[pl.BlockSpec(memory_space=pl.ANY)],
        out_specs=pl.BlockSpec(memory_space=pl.ANY),
        scratch_shapes=[V((2, 6, 256, 256), f), V((128, 256), f)] + [V((256, 768), f)] * 3 + [V((256, 512), f)] * 6
        + [V((256, 128), f)] * 4 + [V((512, 256), f)] * 2
        + [dma((2, 3)), dma((8,)), dma((3, 7)), dma((3, 7)), dma((3,)), dma((4,))],
        compiler_params=pltpu.CompilerParams(vmem_limit_bytes=40 << 20, collective_id=0, has_side_effects=True),
    )(box_operators[:, 0])
    return out[:, None]


def solution(mesh):
    return jax.shard_map(
        per_device,
        mesh=mesh,
        in_specs=(P(None, "box", None, "tile", "col"),),
        out_specs=P(None, "box", "tile", "col"),
        check_vma=False,
    )
```

```python
import jax
import jax.numpy as jnp
from jax import lax
from jax.experimental import pallas as pl
from jax.experimental.pallas import tpu as pltpu
from jax.sharding import PartitionSpec as P

HI = lax.Precision.HIGHEST

def dot(a, b, ca=1, cb=0):
    return lax.dot_general(a, b, (((ca,), (cb,)), ((), ())), precision=HI, preferred_element_type=jnp.float32)

def leaf(cols, sub):
    cols = list(cols)
    scale = None
    for k in range(8):
        piv = 1.0 / jnp.broadcast_to(cols[k][k:k + 1, :], (8, 128))
        here = sub == k
        factors = jnp.where(here, 0.0, cols[k]) * piv
        scale = piv if scale is None else jnp.where(sub >= k, piv, scale)
        for q in range(1, 8):
            c = (k + q) % 8
            cols[c] = cols[c] - factors * jnp.broadcast_to(cols[c][k:k + 1, :], (8, 128))
        cols[k] = jnp.where(here, 1.0, -factors)
    return [c * scale for c in cols]


def treesum(xs):
    while len(xs) > 1:
        xs = [xs[i] + xs[i+1] if i + 1 < len(xs) else xs[i] for i in range(0, len(xs), 2)]
    return xs[0]

def apply8(cols, y):
    return treesum([cols[j] * jnp.broadcast_to(y[j:j+1, :], (8, 128)) for j in range(8)])

PANEL = 4
LOOK = 2


def eliminate(mats, hook=None):
    sub = lax.broadcasted_iota(jnp.int32, (8, 128), 0)
    lane = lax.broadcasted_iota(jnp.int32, (8, 128), 1)
    panel = PANEL if len(mats) > 1 else PANEL // 2
    mats = [list(m) for m in mats]
    es = [[] for _ in mats]
    fs = [[] for _ in mats]
    panels = [[] for _ in mats]
    for k in range(16):
        if hook is not None:
            hook(k)
        lo = 8 * k
        end = k // panel * panel + panel
        inside = (lane >= lo) & (lane < lo + 8)
        eye = jnp.where(lane == sub + lo, 1.0, 0.0).astype(jnp.float32)
        for n, m in enumerate(mats):
            r = m[k]
            cols = leaf([jnp.broadcast_to(r[:, lo + c:lo + c + 1], (8, 128)) for c in range(8)], sub)
            rm = jnp.where(inside, eye, r)
            y = apply8(cols, rm)
            es[n].append(jnp.where(lane < lo + 8, rm, 0.0))
            fs[n].append(jnp.where(lane < lo + 8, y, 0.0))
            panels[n].append((rm, jnp.where((lane >= lo + 8) & (lane < 8 * end), 0.0, y)))
            yb = [jnp.broadcast_to(y[j:j + 1, :], (8, 128)) for j in range(8)]
            for i in range(k + 1, min(end + LOOK, 16)):
                a = m[i]
                m[i] = jnp.where(inside, 0.0, a) - treesum(
                    [jnp.broadcast_to(a[:, lo + j:lo + j + 1], (8, 128)) * yb[j] for j in range(8)])
        if k + 1 == end and end + LOOK < 16:
            gone = (lane >= 8 * (end - panel)) & (lane < 8 * end)
            for n, m in enumerate(mats):
                v = jnp.concatenate([p[0] for p in panels[n]], axis=0)
                y = jnp.concatenate([p[1] for p in panels[n]], axis=0)
                update = dot(v, y, 0, 0)
                for i in range(end + LOOK, 16):
                    m[i] = jnp.where(gone, 0.0, m[i]) - update[8 * i:8 * i + 8, :]
        if k + 1 == end:
            panels = [[] for _ in mats]
    return es, fs


def factor(mat_refs, fac_refs, hook=None):
    es, des = eliminate([[m[8*i:8*i+8, :] for i in range(16)] for m in mat_refs], hook)
    for f, e, d in zip(fac_refs, es, des):
        for i in range(16):
            f[8*i:8*i+8, :] = e[i]
            f[128+8*i:128+8*i+8, :] = d[i]

def dot3(a, b, ca=1, cb=0):
    ah = a.astype(jnp.bfloat16)
    al = (a - ah.astype(jnp.float32)).astype(jnp.bfloat16)
    bh = b.astype(jnp.bfloat16)
    bl = (b - bh.astype(jnp.float32)).astype(jnp.bfloat16)

    def one(p, q):
        return lax.dot_general(p, q, (((ca,), (cb,)), ((), ())), preferred_element_type=jnp.float32)
    return one(ah, bh) + (one(ah, bl) + one(al, bh))


def solve(a, fac, fac2, v, y):
    factor([a.at[0:128, 0:128]], [fac])
    vy = dot(fac[...], a[0:128, 128:256])
    a[128:256, 128:256] = a[128:256, 128:256] - dot(vy[0:128], vy[128:], 0, 0)
    wide = dot3(fac[...], a[0:128, 256:])
    v[0:128, :] = wide[0:128]
    y[0:128, :] = wide[128:]
    a[128:256, 256:] = a[128:256, 256:] - dot3(vy[0:128], wide[128:], 0, 0)
    factor([a.at[128:256, 128:256]], [fac2])
    wide = dot3(fac2[...], a[128:256, 256:])
    v[128:256, :] = wide[0:128]
    y[128:256, :] = wide[128:]


MESH = pl.DeviceIdType.MESH

def kernel(x_ref, out_ref, g, ob, a0, a1, a2, v0, v1, v2, y0, y1, y2, f0, f1, f2, f3, e0, e1,
           send1, recv1, send2, recv2, sendo, recvo):
    box = lax.axis_index("box")
    tile = lax.axis_index("tile")
    col = lax.axis_index("col")
    b = box % 4
    quad = box - b
    core = tile % 2
    x = 2 * col + tile // 2

    def at(dz, dx):
        xx = (x + dx) % 4
        return {"box": quad + (b + dz) % 4, "col": xx // 2, "tile": xx % 2 * 2 + core}

    sib = {"tile": tile + 1 - 2 * core}

    barrier = pltpu.get_barrier_semaphore()
    for dev in [at(d, 0) for d in (1, 2, 3)] + [at(0, d) for d in (1, 2, 3)] + [sib]:
        pl.semaphore_signal(barrier, inc=1, device_id=dev, device_id_type=MESH)
    pl.semaphore_wait(barrier, 7)

    def remote(src, dst, s, r, dev):
        return pltpu.make_async_remote_copy(src_ref=src, dst_ref=dst, send_sem=s, recv_sem=r,
                                            device_id=dev, device_id_type=MESH)

    def wait_for(p, sem):
        pltpu.make_async_copy(p, p, sem).wait()

    def rows_of(t):
        return pl.ds(pl.multiple_of(t * 64, 64), 64)

    rows = rows_of(tile)
    LO, HI_, ALL = pl.ds(0, 128), pl.ds(128, 128), pl.ds(0, 256)

    is_s = col != b % 2
    is_w = jnp.logical_not(is_s)
    is_top = tile // 2 == 0
    is_bottom = tile // 2 == 1
    own_slot = jnp.where((b == 1) | (b == 2), 4, 5)

    def first(kind, face, slot, cs, sem):
        dst = g.at[col, slot, rows, cs]
        away = [remote(x_ref.at[(b + d) % 4, face, :, cs], dst, send1.at[kind, d - 1], recv1.at[sem], at(d, 0))
                for d in (1, 3, 2)]
        return away, lambda: pltpu.make_async_copy(x_ref.at[b, face, :, cs], dst, recv1.at[sem])

    def first_a():
        return first(0, col, b // 2, LO, 6 + b // 2)

    def first_b():
        return first(1, col, b // 2, HI_, b // 2)

    def first_w():
        return first(0, 1 - col, 2 + b // 2, ALL, 2 + b // 2)

    def first_own():
        return first(1, col, own_slot, ALL, own_slot)

    def begin(cond, *makers):
        @pl.when(cond)
        def _():
            for maker in makers:
                away, home = maker()
                for c in away:
                    c.start()
                home().start()

    def sent(cond, *makers):
        @pl.when(cond)
        def _():
            for maker in makers:
                for c in maker()[0]:
                    c.wait_send()

    A, B, W = range(3)
    SLOTS = (pl.ds(0, 2), pl.ds(0, 2), pl.ds(2, 3))
    CS = (LO, HI_, ALL)
    SEMS = (((0, 6), (1, 7)), ((0, 0), (1, 1)), ((2, 2), (3, 3), (4, 4)))
    pending = []

    def under(cond, fn):
        if cond is None:
            fn()
        else:
            pl.when(cond)(fn)

    def piece(unit, d, other=0):
        xx = (x + d) % 4
        t = xx % 2 * 2 + core + other * (1 - 2 * core)
        return g.at[xx // 2, SLOTS[unit], rows_of(t), CS[unit]]

    def ring_copy(unit, src, n):
        p = piece(unit, src)
        return remote(p, p, send2.at[unit, n], recv2.at[unit, n], at(0, n) if n in (1, 2, 3) else sib)

    def go(cond, *args):
        ring_copy(*args).start()
        pending.append((cond, args))

    def have(unit, d):
        return None if unit != A else is_top if d % 2 == 0 else is_bottom

    def ring_start(unit):
        cond = have(unit, 0)

        def do():
            for slot, sem in SEMS[unit]:
                wait_for(g.at[col, slot, rows, CS[unit]], recv1.at[sem])
            for d in (2, 1, 3):
                go(cond, unit, 0, d)
            go(cond, unit, 0, 0)
        under(cond, do)

    def ring_share(unit, ds=(1, 3, 2)):
        for d in ds:
            cond = have(unit, d)

            def do():
                wait_for(piece(unit, 4 - d), recv2.at[unit, d])
                go(cond, unit, 4 - d, 3 + d)
            under(cond, do)

    def ring_done(unit):
        under(have(unit, 0), lambda: wait_for(piece(unit, 0, 1), recv2.at[unit, 0]))
        for d in (1, 3, 2):
            under(have(unit, d), lambda: wait_for(piece(unit, 4 - d, 1), recv2.at[unit, 3 + d]))

    begin(is_s & is_top, first_a)
    begin(is_s, first_b)
    begin(is_w & is_bottom, first_w, first_own)
    ring_start(A)
    begin(is_w & is_top, first_w, first_own)
    ring_share(A)
    ring_start(B)
    ring_done(A)
    ring_start(W)

    during_first = {}
    during_second = {}

    def hook(table):
        return lambda k: table[k]() if k in table else None

    for p, a in enumerate((a0, a1)):
        a[0:128, 0:128] = g[0, p, 0:128, 0:128] + g[1, p, 0:128, 0:128]
    factor([a.at[0:128, 0:128] for a in (a0, a1)], [f0, f1], hook(during_first))
    ring_share(B)
    ring_done(B)
    for p, (a, f) in enumerate(((a0, f0), (a1, f1))):
        vy = dot(f[...], g[0, p, 0:128, 128:256] + g[1, p, 0:128, 128:256])
        a[0:128, 0:128] = vy[0:128]
        a[128:256, 128:256] = g[0, p, 128:256, 128:256] + g[1, p, 128:256, 128:256] - dot(vy[0:128], vy[128:], 0, 0)
    factor([a.at[128:256, 128:256] for a in (a0, a1)], [f2, f3], hook(during_second))
    ring_share(W)
    for a, f, h, ef in ((a0, f0, f2, e0), (a1, f1, f3, e1)):
        low = dot3(h[...], -dot3(a[0:128, 0:128], f[128:256, :], 0, 0))
        ef[0:128, 0:128] = f[0:128, :]
        ef[0:128, 128:256] = jnp.zeros((128, 128), jnp.float32)
        ef[128:256, 0:128] = low[0:128]
        ef[128:256, 128:256] = h[0:128, :]
        ef[256:384, 0:128] = f[128:256, :]
        ef[256:384, 128:256] = jnp.zeros((128, 128), jnp.float32)
        ef[384:512, 0:128] = low[128:]
        ef[384:512, 128:256] = h[128:256, :]
    ring_done(W)
    for p, (ef, v, y) in enumerate(((e0, v0, y0), (e1, v1, y1))):
        for c in (1 - p, p):
            vy = dot3(ef[...], g[c, 2 + p])
            v[:, 256 * c:256 * c + 256] = vy[0:256]
            y[:, 256 * c:256 * c + 256] = vy[256:512]

    a2[:, 0:256] = (g[0, 4] + g[1, 4] - dot3(v0[:, 256:512], y0[:, 256:512], 0, 0)
                    - dot3(v1[:, 0:256], y1[:, 0:256], 0, 0))
    a2[:, 256:512] = -dot3(v0[:, 256:512], y0[:, 0:256], 0, 0)
    a2[:, 512:768] = -dot3(v1[:, 0:256], y1[:, 256:512], 0, 0)

    start = pl.multiple_of(tile // 2 * 128, 128)
    cols = pl.multiple_of(col * 256, 256)
    a1[:, 0:128] = jnp.where(col == 0, v0[:, pl.ds(start, 128)], v1[:, pl.ds(start + 256, 128)])
    a1[:, 256:512] = jnp.where(col == 0, y0[:, 0:256], y1[:, 256:512])
    a0[0:128, 512:768] = dot3(a1[:, 0:128], a1[:, 256:512], 0, 0)
    solve(a2, f0, f1, v2, y2)

    a0[:, 0:128] = v2[:, pl.ds(start, 128)]
    a0[:, 128:256] = v2[:, pl.ds(start + 256, 128)]
    a0[:, 256:512] = y2[:, pl.ds(cols, 256)]
    a2[:, 0:256] = dot3(a0[:, 0:256], a0[:, 256:512], 0, 0)
    row = pl.multiple_of(core * 64, 64)
    wait_for(g.at[col, 5, rows, :], recv1.at[5])
    own = g[col, 5, rows, :] - a0[pl.ds(row, 64), 512:768]
    ob[0:64, :] = jnp.where(col == 0, own, 0.0) - a2[pl.ds(row, 64), 0:256]
    ob[64:128, :] = jnp.where(col == 1, own, 0.0) - a2[pl.ds(128 + row, 64), 0:256]

    def result(to):
        return ob.at[pl.ds(pl.multiple_of(to * 32, 32), 32), :]

    outs = [remote(result((b + d) % 4), out_ref.at[b], sendo.at[d - 1], recvo.at[d - 1], at(d, 0)) for d in (1, 2, 3)]
    for c in outs:
        c.start()
    home = pltpu.make_async_copy(result(b), out_ref.at[b], recvo.at[3])
    home.start()
    for c in outs:
        c.wait_send()
    for d in (1, 2, 3):
        wait_for(out_ref.at[(b + 4 - d) % 4], recvo.at[d - 1])
    home.wait()
    for cond in (None, is_top, is_bottom):
        def drain():
            for c, args in pending:
                if c is cond:
                    ring_copy(*args).wait_send()
        under(cond, drain)
    sent(is_s & is_top, first_a)
    sent(is_s, first_b)
    sent(is_w, first_w, first_own)


def per_device(box_operators):
    V = pltpu.VMEM
    f = jnp.float32
    dma = pltpu.SemaphoreType.DMA
    out = pl.pallas_call(
        kernel,
        out_shape=jax.ShapeDtypeStruct((4, 32, 256), f),
        in_specs=[pl.BlockSpec(memory_space=pl.ANY)],
        out_specs=pl.BlockSpec(memory_space=pl.ANY),
        scratch_shapes=[V((2, 6, 256, 256), f), V((128, 256), f)] + [V((256, 768), f)] * 3 + [V((256, 512), f)] * 6
        + [V((256, 128), f)] * 4 + [V((512, 256), f)] * 2
        + [dma((2, 3)), dma((8,)), dma((3, 7)), dma((3, 7)), dma((3,)), dma((4,))],
        compiler_params=pltpu.CompilerParams(vmem_limit_bytes=40 << 20, collective_id=0, has_side_effects=True),
    )(box_operators[:, 0])
    return out[:, None]


def solution(mesh):
    return jax.shard_map(
        per_device,
        mesh=mesh,
        in_specs=(P(None, "box", None, "tile", "col"),),
        out_specs=P(None, "box", "tile", "col"),
        check_vma=False,
    )
```
